32 devices in a mesh: parts: 2 (over y), clus: 4 (over z), mem: 2 (over x), sub: 2 (over core).
Axes of the slice: x: 2, y: 2, z: 4, core: 2. Of those that a mesh axis runs over, the one named last changes fastest.
Arguments:
- embeddings: bfloat16 [4096, 1024], P(('parts', 'clus', 'mem', 'sub')), parts along dimension 0, as said below
- labels: int32 [4096], P(('parts', 'clus', 'mem', 'sub')), parts along dimension 0, may hold values from 0 to 15, as said below
- member_rank: int32 [4096], P(('parts', 'clus', 'mem', 'sub')), parts along dimension 0, may hold values from 0 to 2047, each once
Outputs:
- nearest: float32 [4096], P(('parts', 'clus', 'mem', 'sub')), parts along dimension 0
The draws below stay inside these ranges and needn't reach their ends.
There are 2 independent parts, one for each index of `parts`. The reference program is written for one: setup_inputs(seed, part) draws one part's arguments, and reference() takes and returns one part's arrays. A program takes and returns all parts, laid end to end along the dimension named above; each array names one. Nothing has to cross between parts.
Inputs may be any that keep to these rules, and one draw needn't show every extreme that they name: `embeddings`: each row has unit length up to rounding. Among the rows of one device, at most 32 have labels in any one group of 2 consecutive clusters (label // 2); on every device some group has exactly 32.
All inputs are finite; a program needn't handle non-finite values.
Results may differ from the reference program's by a relative error of at most 0.0003.
Values may be sent and summed in bfloat16 or wider, within the bound.
A program may use at most 64 MiB of HBM per device.

```python
import jax
import jax.numpy as jnp
from jax import lax

D = 1024
ROWS_DEV = 128
CLUS_GROUP = 2
GROUPS = 8
CAPACITY = 32
SLOTS = 256
SHARDS = 16
MEMBERS = 2048
CLUSTERS = 16


def member_layout(key):
    base = jax.random.fold_in(key, 11)
    key_full, key_score, key_shuffle, key_first, key_second = jax.random.split(base, 5)
    full_group = jax.random.randint(key_full, (SHARDS,), 0, GROUPS)
    scores = jax.random.randint(key_score, (SHARDS, SLOTS), 0, 1 << 20)
    slot_group = jnp.arange(SLOTS, dtype=jnp.int32) // CAPACITY
    scores = jnp.where(slot_group[None, :] == full_group[:, None], -1, scores)
    chosen = jnp.argsort(scores, axis=1, stable=True)[:, :ROWS_DEV].astype(jnp.int32)
    shuffle_key = jax.random.randint(key_shuffle, (SHARDS, ROWS_DEV), 0, 1 << 20)
    shuffle_order = jnp.argsort(shuffle_key, axis=1, stable=True)
    chosen = jnp.take_along_axis(chosen, shuffle_order, axis=1)
    within = jnp.minimum(jax.random.randint(key_first, (SHARDS, ROWS_DEV), 0, CLUS_GROUP), jax.random.randint(key_second, (SHARDS, ROWS_DEV), 0, CLUS_GROUP))
    label_all = chosen // CAPACITY * CLUS_GROUP + within
    return label_all.reshape(-1).astype(jnp.int32)


def draw_labels(key, part):
    return member_layout(key)


def draw_embeddings(key, part):
    label_all = member_layout(key)
    key_centre, key_weight, key_noise = jax.random.split(jax.random.fold_in(key, 23), 3)
    centre = jax.random.normal(key_centre, (CLUSTERS, D), jnp.float32)
    centre = centre / jnp.sqrt(jnp.sum(centre * centre, axis=1, keepdims=True))
    weight = jax.random.uniform(key_weight, (MEMBERS, 1), jnp.float32, 0.2, 0.95)
    noise_vec = jax.random.normal(key_noise, (MEMBERS, D), jnp.float32)
    noise_vec = noise_vec / jnp.sqrt(jnp.sum(noise_vec * noise_vec, axis=1, keepdims=True))
    mixed_vec = weight * centre[label_all] + jnp.sqrt(1.0 - weight * weight) * noise_vec
    mixed_vec = mixed_vec / jnp.sqrt(jnp.sum(mixed_vec * mixed_vec, axis=1, keepdims=True))
    return mixed_vec.astype(jnp.bfloat16)


def setup_inputs(seed: int = 0, part: int = 0) -> dict:
    key_list = jax.random.split(jax.random.key(seed), 4)
    own_keys = jax.random.split(jax.random.fold_in(key_list[3], part), 4)
    embeddings = draw_embeddings(jax.random.fold_in(jax.random.fold_in(key_list[3], part), 71), part)
    labels = draw_labels(jax.random.fold_in(jax.random.fold_in(key_list[3], part), 71), part)
    member_rank = jax.random.permutation(own_keys[2], MEMBERS).astype(jnp.int32)
    return dict(embeddings=embeddings, labels=labels, member_rank=member_rank)


def reference(embeddings, labels, member_rank):
    group_of = labels // CLUS_GROUP
    member_count = embeddings.shape[0]
    group_width = SHARDS * CAPACITY

    def per_group(group_id):
        in_group = group_of == group_id
        member_idx = jnp.nonzero(in_group, size=group_width, fill_value=0)[0].astype(jnp.int32)
        live_slot = jnp.arange(group_width) < jnp.sum(in_group)
        slot_emb = embeddings[member_idx]
        slot_label = jnp.where(live_slot, labels[member_idx], -1)
        slot_rank = member_rank[member_idx]
        scores = jnp.dot(slot_emb, slot_emb.T, preferred_element_type=jnp.float32)
        allowed = (slot_label[:, None] == slot_label[None, :]) & (slot_label[:, None] >= 0)
        allowed = allowed & (slot_rank[None, :] < slot_rank[:, None])
        nearest = jnp.max(jnp.where(allowed, scores, jnp.float32(-1.0)), axis=1)
        return jnp.where(live_slot, member_idx, member_count), nearest

    all_idx, all_best = lax.map(per_group, jnp.arange(GROUPS, dtype=jnp.int32))
    result = jnp.full((member_count,), -1.0, jnp.float32)
    return result.at[all_idx.reshape(-1)].set(all_best.reshape(-1), mode="drop")
```

```python
import functools
import math

import jax
import jax.numpy as jnp
from jax import lax
from jax.experimental import pallas as pl
from jax.experimental.pallas import tpu as pltpu
from jax.sharding import PartitionSpec as P

CLUS_GROUP = 2
MESH = pl.DeviceIdType.MESH
LANES = 128
PAIR = 2
PIECES = 4
CLASS_STEP = 65536
EXACT = 2**24


def nt_dot(lhs, rhs):
    return lax.dot_general(lhs, rhs, (((1,), (1,)), ((), ())), preferred_element_type=jnp.float32)


def dedup_kernel(
    emb_hbm,
    label_hbm,
    rank_hbm,
    out_ref,
    side,
    twin,
    far_rows,
    relay,
    key_side,
    key_twin,
    key_far,
    best,
    best_far,
    ret_out,
    ret_in,
    load_sem,
    send_sem,
    recv_sem,
):
    rows, _ = emb_hbm.shape
    chunk = rows // PIECES
    part = lax.axis_index("parts")
    clus = lax.axis_index("clus")
    mem = lax.axis_index("mem")
    sub = lax.axis_index("sub")
    clus_count = lax.axis_size("clus")
    parity = lax.rem(clus, 2)
    along = clus + 1 - 2 * parity
    across = clus_count - 1 - clus
    beyond = clus_count - 1 - along
    is_inner = (clus >= 1) & (clus < clus_count - 1)
    gives = lax.div(clus, 2) != part
    to_along = {"clus": along}
    to_across = {"clus": across}
    to_column = {"mem": 1 - mem}
    to_twin = {"sub": 1 - sub}
    to_part = {"parts": 1 - part}

    used = {}

    def copy(name, src, dst, device):
        slot = used.setdefault(name, len(used))
        return pltpu.make_async_remote_copy(
            src_ref=src,
            dst_ref=dst,
            send_sem=send_sem.at[slot],
            recv_sem=recv_sem.at[slot],
            device_id=device,
            device_id_type=MESH,
        )

    def span(k, count=1):
        return pl.ds(k * chunk, count * chunk)

    def piece(ref, slot, k, count=1):
        return ref.at[slot, span(k, count), :]

    load_label = pltpu.make_async_copy(label_hbm, key_side.at[0, 0], load_sem.at[0])
    load_rank = pltpu.make_async_copy(rank_hbm, key_side.at[0, 1], load_sem.at[1])
    load_rows = pltpu.make_async_copy(emb_hbm, side.at[0], load_sem.at[2])

    half = PIECES // 2
    up = [copy(("up", k), emb_hbm.at[span(k), :], piece(side, 1, k), to_along) for k in range(PIECES)]
    swing = [
        copy(("swing", k), emb_hbm.at[span(k), :], piece(side, 3, k), to_column)
        for k in range(half, PIECES)
    ]
    swing_up = [
        copy(("swing_up", k), piece(side, 3, k), piece(side, 3, k), to_along)
        for k in range(half, PIECES)
    ]
    key_up = [
        copy("label_up", label_hbm, key_side.at[1, 0], to_along),
        copy("rank_up", rank_hbm, key_side.at[1, 1], to_along),
    ]
    wide = [
        copy(("wide", k), emb_hbm.at[span(k), :], piece(side, 2, k), to_column)
        for k in range(PIECES)
    ]
    wide_outer = [
        copy(("wide_outer", k), piece(side, 1, k), piece(side, 3, k), to_column)
        for k in range(half)
    ]
    key_wide = copy("key_wide", key_side.at[pl.ds(0, 2)], key_side.at[pl.ds(2, 2)], to_column)
    pass_own = copy("pass_own", emb_hbm, twin.at[0], to_twin)
    pass_outer = [
        copy(("pass_outer", k), piece(side, 1, k), piece(twin, 1, k), to_twin)
        for k in range(PIECES)
    ]
    key_pass = copy("key_pass", key_side.at[pl.ds(0, 2)], key_twin, to_twin)
    cross_own = [
        copy(("cross_own", k), emb_hbm.at[span(k), :], piece(far_rows, 0, k), to_across)
        for k in range(half, PIECES)
    ]
    cross_outer = [
        copy(("cross_outer", k), piece(side, 1, k), piece(far_rows, 1, k), to_across)
        for k in range(PIECES)
    ]
    key_cross = copy("key_cross", key_side.at[pl.ds(0, 2)], key_far.at[pl.ds(0, 2)], to_across)
    lend = [
        copy(("lend", k), emb_hbm.at[span(k), :], relay.at[span(k), :], to_part)
        for k in range(half)
    ]
    lend_on = [
        copy(
            ("lend_on", k),
            relay.at[span(k), :],
            piece(far_rows, 0, k),
            {"parts": 1 - part, "clus": across},
        )
        for k in range(half)
    ]
    share_own = [
        copy(("share_own", k), piece(far_rows, 0, k), piece(far_rows, 2, k), to_twin)
        for k in range(PIECES)
    ]
    share_outer = [
        copy(("share_outer", k), piece(far_rows, 1, k), piece(far_rows, 3, k), to_twin)
        for k in range(PIECES)
    ]
    key_share = copy("key_share", key_far.at[pl.ds(0, 2)], key_far.at[pl.ds(2, 2)], to_twin)
    back = {
        "outer": copy("back_outer", ret_out.at[1], ret_in.at[0], to_along),
        "inner": copy("back_inner", ret_out.at[2], ret_in.at[1], to_column),
        "outer_wide": copy(
            "back_outer_wide", ret_out.at[3], ret_in.at[1], {"clus": along, "mem": 1 - mem}
        ),
    }
    home = [
        copy("home_0", ret_out.at[4], ret_in.at[2], to_across),
        copy("home_1", ret_out.at[5], ret_in.at[2], {"clus": beyond}),
        copy("home_2", ret_out.at[6], ret_in.at[3], {"clus": across, "sub": 1 - sub}),
        copy("home_3", ret_out.at[7], ret_in.at[3], {"clus": beyond, "sub": 1 - sub}),
    ]

    barrier = pltpu.get_barrier_semaphore()

    def greet(devices):
        for device in devices:
            pl.semaphore_signal(barrier, inc=1, device_id=device, device_id_type=MESH)
        return len(devices)

    def key_of(ref, slot):
        return (ref[slot, 0] * CLASS_STEP + ref[slot, 1]).astype(jnp.float32)

    def cluster(key):
        return jnp.floor(key * (1.0 / CLASS_STEP))

    def column(key_ref, slot):
        return jnp.transpose(jnp.broadcast_to(key_of(key_ref, slot), (LANES, rows)))

    def visit(source, slot, first, count, key_ref, tiles, far_slot=None):
        size = count * chunk
        cand_key = column(key_ref, slot)[first * chunk : first * chunk + size]
        cand_cluster = cluster(cand_key)
        members = side[tiles[0] : tiles[-1] + 1].reshape(len(tiles) * rows, side.shape[2])
        scores = nt_dot(source[slot, span(first, count), :], members)
        reverse = None
        for n, tile in enumerate(tiles):
            score = scores[:, n * rows : (n + 1) * rows]
            member_key = key_of(key_side, tile)
            same = cand_cluster == cluster(member_key)
            earlier = same & (cand_key < member_key)
            top = jnp.max(jnp.where(earlier, score, -1.0), axis=0, keepdims=True)
            best[tile] = jnp.maximum(best[tile], top)
            if far_slot is not None:
                later = jnp.where(same & (cand_key > member_key), score, -1.0)
                reverse = later if reverse is None else jnp.maximum(reverse, later)
        if far_slot is not None:
            part_rows = span(first, count)
            best_far[far_slot, part_rows, :] = jnp.maximum(
                best_far[far_slot, part_rows, :], reverse
            )

    def open_inner(gives_here):
        load_label.start()
        load_rank.start()
        load_rows.start()
        met = greet([to_along, to_across, to_column, to_twin, to_part])
        best[...] = jnp.full(best.shape, -1.0, jnp.float32)
        pl.semaphore_wait(barrier, met)
        if gives_here:
            for c in lend + cross_own:
                c.start()
        for c in wide:
            c.start()
        pass_own.start()
        load_label.wait()
        load_rank.wait()
        for c in key_up:
            c.wait_recv()
        key_pass.start()
        key_wide.start()
        if gives_here:
            key_cross.start()

    def outer_arrived(k, gives_here):
        up[k].wait_recv()
        if gives_here:
            cross_outer[k].start()
        if k < half:
            wide_outer[k].start()
        pass_outer[k].start()

    def settle(copies):
        for c in copies:
            c.wait_recv()

    inner_sent = wide + wide_outer + pass_outer + [pass_own, key_wide, key_pass]

    def result(slots):
        value = ret_in[slots[0]]
        for slot in slots[1:]:
            value = jnp.maximum(value, ret_in[slot])
        return value

    near_tiles = [0, 1, 2]
    last_tile = [3]

    @pl.when(jnp.logical_not(is_inner))
    def _():
        met = greet([to_along, to_column])
        pl.semaphore_wait(barrier, met)
        for c in key_up + up + swing:
            c.start()
        for c, onward in zip(swing, swing_up, strict=True):
            c.wait_recv()
            onward.start()
        back["outer"].wait_recv()
        back["outer_wide"].wait_recv()

        @pl.when(gives)
        def _():
            home[1].wait_recv()
            home[3].wait_recv()
            out_ref[...] = result([0, 1, 2, 3])

        @pl.when(jnp.logical_not(gives))
        def _():
            out_ref[...] = result([0, 1])

        for c in key_up + up + swing + swing_up:
            c.wait_send()

    @pl.when(is_inner & gives)
    def _():
        open_inner(True)
        for k in range(PIECES):
            outer_arrived(k, True)
        load_rows.wait()
        settle([key_wide, key_pass, pass_own] + pass_outer + wide)
        for slot in range(2):
            visit(side, slot, 0, PIECES, key_side, near_tiles)
            visit(twin, slot, 0, PIECES, key_twin, near_tiles)
        for tile in near_tiles[1:]:
            ret_out[tile] = best[tile]
        back["outer"].start()
        back["inner"].start()
        settle(wide_outer + swing_up)
        for slot in range(2):
            visit(side, slot, 0, PIECES, key_side, last_tile)
            visit(twin, slot, 0, PIECES, key_twin, last_tile)
        ret_out[3] = best[3]
        back["outer_wide"].start()
        back["inner"].wait_recv()
        home[0].wait_recv()
        home[2].wait_recv()
        out_ref[...] = jnp.maximum(best[0], result([1, 2, 3]))
        for c in inner_sent + lend + cross_own + cross_outer + [key_cross] + list(back.values()):
            c.wait_send()

    @pl.when(is_inner & jnp.logical_not(gives))
    def _():
        best_far[...] = jnp.full(best_far.shape, -1.0, jnp.float32)
        open_inner(False)
        for k in range(half):
            outer_arrived(k, False)
            lend[k].wait_recv()
            lend_on[k].start()
            cross_own[k].wait_recv()
            share_own[half + k].start()
        outer_arrived(2, False)
        key_cross.wait_recv()
        key_share.start()
        cross_outer[0].wait_recv()
        share_outer[0].start()
        outer_arrived(3, False)
        cross_outer[1].wait_recv()
        share_outer[1].start()
        load_rows.wait()
        settle([key_wide, key_pass, pass_own] + pass_outer + wide)
        for slot in range(2):
            visit(side, slot, 0, PIECES, key_side, near_tiles)
            visit(twin, slot, 0, PIECES, key_twin, near_tiles)
        for k in range(half):
            lend_on[k].wait_recv()
            share_own[k].start()
        cross_outer[2].wait_recv()
        share_outer[2].start()
        key_share.wait_recv()
        visit(far_rows, 0, 0, PIECES, key_far, near_tiles, 0)
        settle(share_own)
        visit(far_rows, 2, 0, PIECES, key_far, near_tiles, 2)
        cross_outer[3].wait_recv()
        share_outer[3].start()
        visit(far_rows, 1, 0, PIECES, key_far, near_tiles, 1)
        settle(wide_outer + swing_up)
        for slot in range(2):
            visit(side, slot, 0, PIECES, key_side, last_tile)
            visit(twin, slot, 0, PIECES, key_twin, last_tile)
        for slot in range(3):
            visit(far_rows, slot, 0, PIECES, key_far, last_tile, slot)
        for slot in range(3):
            ret_out[4 + slot] = jnp.max(jnp.transpose(best_far[slot]), axis=0, keepdims=True)
        for c in home[:3]:
            c.start()
        settle(share_outer)
        visit(far_rows, 3, 0, PIECES, key_far, near_tiles + last_tile, 3)
        for tile in near_tiles[1:] + last_tile:
            ret_out[tile] = best[tile]
        for c in back.values():
            c.start()
        ret_out[7] = jnp.max(jnp.transpose(best_far[3]), axis=0, keepdims=True)
        home[3].start()
        back["inner"].wait_recv()
        out_ref[...] = jnp.maximum(best[0], result([1]))
        for c in inner_sent + lend_on + share_own + share_outer + [key_share] + home + list(back.values()):
            c.wait_send()


COPIES = 64


def kernel_body(embeddings, labels, member_rank):
    rows, width = embeddings.shape
    chunk = rows // PIECES
    dma = pltpu.SemaphoreType.DMA
    kept = embeddings.dtype
    out = pl.pallas_call(
        dedup_kernel,
        out_shape=jax.ShapeDtypeStruct((1, rows), jnp.float32),
        in_specs=[pl.BlockSpec(memory_space=pl.ANY)] * 3,
        out_specs=pl.BlockSpec(memory_space=pltpu.VMEM),
        scratch_shapes=[
            pltpu.VMEM((4, rows, width), kept),
            pltpu.VMEM((2, rows, width), kept),
            pltpu.VMEM((4, rows, width), kept),
            pltpu.VMEM((rows // 2, width), kept),
            pltpu.VMEM((4, 2, 1, rows), jnp.int32),
            pltpu.VMEM((2, 2, 1, rows), jnp.int32),
            pltpu.VMEM((4, 2, 1, rows), jnp.int32),
            pltpu.VMEM((4, 1, rows), jnp.float32),
            pltpu.VMEM((4, rows, rows), jnp.float32),
            pltpu.VMEM((8, 1, rows), jnp.float32),
            pltpu.VMEM((4, 1, rows), jnp.float32),
            dma((3,)),
            dma((COPIES,)),
            dma((COPIES,)),
        ],
        compiler_params=pltpu.CompilerParams(collective_id=0, has_side_effects=True),
    )(embeddings, labels.reshape(1, rows), member_rank.reshape(1, rows))
    return out.reshape(rows)


def fits_kernel(rows):
    parts, clus, mem, sub = (lax.axis_size(a) for a in ("parts", "clus", "mem", "sub"))
    members = rows * clus * mem * sub
    clusters = CLUS_GROUP * clus * mem
    return (
        parts == mem == sub == PAIR
        and clus == 2 * PAIR
        and rows == LANES
        and members <= CLASS_STEP
        and clusters * CLASS_STEP <= EXACT
    )


def swapped(value, axis, stride):
    mask = 2**stride
    pairs = [(source, source ^ mask) for source in range(lax.axis_size(axis))]
    return lax.ppermute(value, axis, pairs)


def masked_best(row_emb, row_label, row_rank, col_emb, col_label, col_rank, want_columns):
    col_count = col_emb.shape[0]
    block_size = math.gcd(512, col_count)
    block_count = col_count // block_size
    emb_blocks = col_emb.reshape(block_count, block_size, col_emb.shape[1])
    label_blocks = col_label.reshape(block_count, block_size)
    rank_blocks = col_rank.reshape(block_count, block_size)

    def visit_block(running, column_piece):
        piece_emb, piece_label, piece_rank = column_piece
        scores = lax.dot_general(
            row_emb, piece_emb, (((1,), (1,)), ((), ())), preferred_element_type=jnp.float32
        )
        same_cluster = (row_label[:, None] == piece_label[None, :]) & (row_label[:, None] >= 0)
        earlier = piece_rank[None, :] < row_rank[:, None]
        row_best = jnp.max(jnp.where(same_cluster & earlier, scores, jnp.float32(-1.0)), axis=1)
        if want_columns:
            later = same_cluster & jnp.logical_not(earlier)
            col_best = jnp.max(jnp.where(later, scores, jnp.float32(-1.0)), axis=0)
        else:
            col_best = jnp.zeros((0,), jnp.float32)
        return (jnp.maximum(running, row_best), col_best)

    initial = jnp.full((row_emb.shape[0],), -1.0, jnp.float32)
    row_best, col_blocks = lax.scan(visit_block, initial, (emb_blocks, label_blocks, rank_blocks))
    return (row_best, col_blocks.reshape(-1))


def body(embeddings, labels, member_rank):
    row_count = embeddings.shape[0]
    feature_count = embeddings.shape[1]
    clus_count = lax.axis_size("clus")
    mem_count = lax.axis_size("mem")
    group_count = clus_count * mem_count
    capacity = 2 * row_count // group_count
    slot_count = group_count * capacity
    group_of = labels // CLUS_GROUP
    one_hot = (group_of[:, None] == jnp.arange(group_count, dtype=jnp.int32)[None, :]).astype(
        jnp.int32
    )
    running_count = jnp.cumsum(one_hot, axis=0) - 1
    within_group = jnp.sum(one_hot * running_count, axis=1)
    slot_of = group_of * capacity + within_group
    send_emb = jnp.zeros((slot_count, feature_count), jnp.bfloat16).at[slot_of].set(embeddings)
    send_label = jnp.full((slot_count,), -1, jnp.int32).at[slot_of].set(labels)
    send_rank = jnp.zeros((slot_count,), jnp.int32).at[slot_of].set(member_rank)
    received = (
        lax.all_to_all(
            send_emb.reshape(group_count, capacity, feature_count),
            ("clus", "mem"),
            split_axis=0,
            concat_axis=0,
            tiled=True,
        ),
        lax.all_to_all(
            send_label.reshape(group_count, capacity),
            ("clus", "mem"),
            split_axis=0,
            concat_axis=0,
            tiled=True,
        ),
        lax.all_to_all(
            send_rank.reshape(group_count, capacity),
            ("clus", "mem"),
            split_axis=0,
            concat_axis=0,
            tiled=True,
        ),
    )
    own_emb = received[0].reshape(slot_count, feature_count)
    own_label = received[1].reshape(slot_count)
    own_rank = received[2].reshape(slot_count)
    other_emb, other_label, other_rank = swapped((own_emb, own_label, own_rank), "sub", 0)
    diag_best, ignored = masked_best(
        own_emb, own_label, own_rank, own_emb, own_label, own_rank, False
    )
    core_side = lax.axis_index("sub")
    is_zero = core_side == 0
    zero_emb = jnp.where(is_zero, own_emb, other_emb)
    zero_label = jnp.where(is_zero, own_label, other_label)
    zero_rank = jnp.where(is_zero, own_rank, other_rank)
    one_emb = jnp.where(is_zero, other_emb, own_emb)
    one_label = jnp.where(is_zero, other_label, own_label)
    one_rank = jnp.where(is_zero, other_rank, own_rank)
    half_count = slot_count // 2
    offset = core_side * half_count
    part_emb = lax.dynamic_slice_in_dim(zero_emb, offset, half_count, 0)
    part_label = lax.dynamic_slice_in_dim(zero_label, offset, half_count, 0)
    part_rank = lax.dynamic_slice_in_dim(zero_rank, offset, half_count, 0)
    half_best, col_part = masked_best(
        part_emb, part_label, part_rank, one_emb, one_label, one_rank, True
    )
    got_half, got_cols = swapped((half_best, col_part), "sub", 0)
    row_side = jnp.concatenate([half_best, got_half])
    cross_best = jnp.where(is_zero, row_side, jnp.maximum(col_part, got_cols))
    nearest = jnp.maximum(diag_best, cross_best)
    returned = lax.all_to_all(
        nearest.reshape(group_count, capacity),
        ("clus", "mem"),
        split_axis=0,
        concat_axis=0,
        tiled=True,
    )
    return returned.reshape(-1)[slot_of]


def local(embeddings, labels, member_rank):
    if fits_kernel(embeddings.shape[0]):
        return kernel_body(embeddings, labels, member_rank)
    return body(embeddings, labels, member_rank)


def solution(mesh):
    placed = (
        P(("parts", "clus", "mem", "sub"), None),
        P(("parts", "clus", "mem", "sub")),
        P(("parts", "clus", "mem", "sub")),
    )
    return jax.shard_map(
        local,
        mesh=mesh,
        in_specs=placed,
        out_specs=P(("parts", "clus", "mem", "sub")),
        check_vma=False,
    )
```

```python
import functools
import math

import jax
import jax.numpy as jnp
from jax import lax
from jax.experimental import pallas as pl
from jax.experimental.pallas import tpu as pltpu
from jax.sharding import PartitionSpec as P

CLUS_GROUP = 2
MESH = pl.DeviceIdType.MESH
LANES = 128
PAIR = 2
PIECES = 8
CLASS_STEP = 65536
EXACT = 2**24


def nt_dot(lhs, rhs):
    return lax.dot_general(lhs, rhs, (((1,), (1,)), ((), ())), preferred_element_type=jnp.float32)


def dedup_kernel(
    emb_hbm,
    label_hbm,
    rank_hbm,
    out_ref,
    side,
    twin,
    far_rows,
    relay,
    key_side,
    key_twin,
    key_far,
    best,
    best_far,
    ret_out,
    ret_in,
    key_column,
    entered,
    load_sem,
    send_sem,
    recv_sem,
):
    rows, _ = emb_hbm.shape
    chunk = rows // PIECES
    part = lax.axis_index("parts")
    clus = lax.axis_index("clus")
    mem = lax.axis_index("mem")
    sub = lax.axis_index("sub")
    clus_count = lax.axis_size("clus")
    parity = lax.rem(clus, 2)
    along = clus + 1 - 2 * parity
    across = clus_count - 1 - clus
    beyond = clus_count - 1 - along
    is_inner = (clus >= 1) & (clus < clus_count - 1)
    gives = lax.div(clus, 2) != part
    to_along = {"clus": along}
    to_across = {"clus": across}
    to_column = {"mem": 1 - mem}
    to_twin = {"sub": 1 - sub}
    to_part = {"parts": 1 - part}

    used = {}

    def copy(name, src, dst, device):
        slot = used.setdefault(name, len(used))
        return pltpu.make_async_remote_copy(
            src_ref=src,
            dst_ref=dst,
            send_sem=send_sem.at[slot],
            recv_sem=recv_sem.at[slot],
            device_id=device,
            device_id_type=MESH,
        )

    def span(k, count=1):
        return pl.ds(k * chunk, count * chunk)

    def piece(ref, slot, k, count=1):
        return ref.at[slot, span(k, count), :]

    load_label = pltpu.make_async_copy(label_hbm, key_side.at[0, 0], load_sem.at[0])
    load_rank = pltpu.make_async_copy(rank_hbm, key_side.at[0, 1], load_sem.at[1])
    load_rows = pltpu.make_async_copy(emb_hbm, side.at[0], load_sem.at[2])

    half = PIECES // 2
    steps = [(0, 2), (2, 2), (4, 2), (6, 1), (7, 1)]
    low_steps = steps[:2]
    high_steps = [(4, 2), (6, 2)]

    def rows_of(step):
        return emb_hbm.at[span(*step), :]

    key_up = [
        copy("label_up", label_hbm, key_side.at[1, 0], to_along),
        copy("rank_up", rank_hbm, key_side.at[1, 1], to_along),
    ]
    up = [copy(("up", t), rows_of(t), piece(side, 1, *t), to_along) for t in steps]
    swing = [copy(("swing", t), rows_of(t), piece(side, 3, *t), to_column) for t in high_steps]
    swing_up = [
        copy(("swing_up", t), piece(side, 3, *t), piece(side, 3, *t), to_along) for t in high_steps
    ]
    wide = copy("wide", emb_hbm, side.at[2], to_column)
    wide_outer = [
        copy(("wide_outer", t), piece(side, 1, *t), piece(side, 3, *t), to_column)
        for t in low_steps
    ]
    key_wide = copy("key_wide", key_side.at[pl.ds(0, 2)], key_side.at[pl.ds(2, 2)], to_column)
    pass_own = copy("pass_own", emb_hbm, twin.at[0], to_twin)
    pass_outer = [
        copy(("pass_outer", t), piece(side, 1, *t), piece(twin, 1, *t), to_twin) for t in steps
    ]
    key_pass = copy("key_pass", key_side.at[pl.ds(0, 2)], key_twin, to_twin)
    upper = (half, half)
    lower = (0, half)
    cross_own = copy("cross_own", rows_of(upper), piece(far_rows, 0, *upper), to_across)
    cross_outer = [
        copy(("cross_outer", t), piece(side, 1, *t), piece(far_rows, 1, *t), to_across)
        for t in steps
    ]
    key_cross = copy("key_cross", key_side.at[pl.ds(0, 2)], key_far.at[pl.ds(0, 2)], to_across)
    lend = [copy(("lend", t), rows_of(t), relay.at[span(*t), :], to_part) for t in low_steps]
    lend_on = [
        copy(
            ("lend_on", t),
            relay.at[span(*t), :],
            piece(far_rows, 0, *t),
            {"parts": 1 - part, "clus": across},
        )
        for t in low_steps
    ]
    share_own = [
        copy(("share_own", t), piece(far_rows, 0, *t), piece(far_rows, 2, *t), to_twin)
        for t in (lower, upper)
    ]
    share_outer = [
        copy(("share_outer", t), piece(far_rows, 1, *t), piece(far_rows, 3, *t), to_twin)
        for t in steps
    ]
    key_share = copy("key_share", key_far.at[pl.ds(0, 2)], key_far.at[pl.ds(2, 2)], to_twin)
    back = {
        "outer": copy("back_outer", ret_out.at[1], ret_in.at[0], to_along),
        "inner": copy("back_inner", ret_out.at[2], ret_in.at[1], to_column),
        "outer_wide": copy(
            "back_outer_wide", ret_out.at[3], ret_in.at[1], {"clus": along, "mem": 1 - mem}
        ),
    }
    home = [
        copy("home_0", ret_out.at[4], ret_in.at[2], to_across),
        copy("home_1", ret_out.at[5], ret_in.at[2], {"clus": beyond}),
        copy("home_2", ret_out.at[6], ret_in.at[3], {"clus": across, "sub": 1 - sub}),
        copy("home_3", ret_out.at[7], ret_in.at[3], {"clus": beyond, "sub": 1 - sub}),
    ]

    barrier = pltpu.get_barrier_semaphore()

    def greet(devices):
        for device in devices:
            pl.semaphore_signal(barrier, inc=1, device_id=device, device_id_type=MESH)
        return len(devices)

    def key_of(ref, slot):
        return (ref[slot, 0] * CLASS_STEP + ref[slot, 1]).astype(jnp.float32)

    def cluster(key):
        return jnp.floor(key * (1.0 / CLASS_STEP))

    def columns(first, ref, slots):
        for n in range(slots):
            key = jnp.broadcast_to(key_of(ref, n), (LANES, rows))
            key_column[first + n] = jnp.transpose(key)

    def visit(source, slot, first_key, step, tiles, reversed_too=False):
        place = span(*step)
        cand_key = key_column[first_key + slot, place, :]
        cand_cluster = cluster(cand_key)
        members = side[tiles[0] : tiles[-1] + 1].reshape(len(tiles) * rows, side.shape[2])
        scores = nt_dot(source[slot, place, :], members)
        reverse = None
        for n, tile in enumerate(tiles):
            score = scores[:, n * rows : (n + 1) * rows]
            member_key = key_of(key_side, tile)
            same = cand_cluster == cluster(member_key)
            earlier = same & (cand_key < member_key)
            top = jnp.max(jnp.where(earlier, score, -1.0), axis=0, keepdims=True)
            best[tile] = jnp.maximum(best[tile], top)
            if reversed_too:
                later = jnp.where(same & (cand_key > member_key), score, -1.0)
                reverse = later if reverse is None else jnp.maximum(reverse, later)
        if reversed_too:
            best_far[slot, place, :] = jnp.maximum(best_far[slot, place, :], reverse)

    def visit_far(slot, step, tiles):
        visit(far_rows, slot, 4, step, tiles, True)

    def visit_half(tiles):
        for slot in range(2):
            visit(side, slot, 0, whole, tiles)
            visit(twin, slot, 2, whole, tiles)

    def open_inner(gives_here):
        load_label.start()
        load_rank.start()
        load_rows.start()
        met = greet([to_along, to_across, to_column, to_twin, to_part])
        best[...] = jnp.full(best.shape, -1.0, jnp.float32)
        pl.semaphore_wait(barrier, met)
        pl.semaphore_signal(entered.at[0], inc=1, device_id=to_column, device_id_type=MESH)
        if gives_here:
            cross_own.start()
            for c in lend:
                c.start()
        wide.start()
        pass_own.start()
        pl.semaphore_wait(entered.at[0], 1)
        pl.semaphore_signal(entered.at[1], inc=1, device_id=to_along, device_id_type=MESH)
        load_label.wait()
        load_rank.wait()
        settle(key_up)
        if gives_here:
            key_cross.start()
        key_pass.start()
        key_wide.start()

    def outer_arrived(n, gives_here):
        up[n].wait_recv()
        if gives_here:
            cross_outer[n].start()
        if n < len(low_steps):
            wide_outer[n].start()
        pass_outer[n].start()

    def settle(copies):
        for c in copies:
            c.wait_recv()

    inner_sent = wide_outer + pass_outer + [wide, pass_own, key_wide, key_pass]
    whole = (0, PIECES)

    def result(slots):
        value = ret_in[slots[0]]
        for slot in slots[1:]:
            value = jnp.maximum(value, ret_in[slot])
        return value

    def send_home(slot):
        ret_out[4 + slot] = jnp.max(jnp.transpose(best_far[slot]), axis=0, keepdims=True)
        home[slot].start()

    near_tiles = [0, 1, 2]
    last_tile = [3]
    all_tiles = near_tiles + last_tile

    def send_back():
        for tile, name in ((3, "outer_wide"), (1, "outer"), (2, "inner")):
            ret_out[tile] = best[tile]
            back[name].start()

    @pl.when(jnp.logical_not(is_inner))
    def _():
        met = greet([to_along])
        pl.semaphore_wait(barrier, met)
        for c in key_up + up:
            c.start()
        pl.semaphore_wait(entered.at[1], 1)
        for c in swing:
            c.start()
        for c, onward in zip(swing, swing_up, strict=True):
            c.wait_recv()
            onward.start()
        for c in key_up + up + swing + swing_up:
            c.wait_send()
        back["outer"].wait_recv()
        back["outer_wide"].wait_recv()

        @pl.when(gives)
        def _():
            home[1].wait_recv()
            home[3].wait_recv()
            out_ref[...] = result([0, 1, 2, 3])

        @pl.when(jnp.logical_not(gives))
        def _():
            out_ref[...] = result([0, 1])

    @pl.when(is_inner & gives)
    def _():
        open_inner(True)
        for n in range(len(steps)):
            outer_arrived(n, True)
        load_rows.wait()
        settle([key_wide, key_pass, pass_own, wide] + pass_outer)
        columns(0, key_side, 2)
        columns(2, key_twin, 2)
        settle(wide_outer + swing_up)
        visit_half(all_tiles)
        send_back()
        for c in inner_sent + lend + cross_outer + [cross_own, key_cross]:
            c.wait_send()
        back["inner"].wait_recv()
        home[0].wait_recv()
        home[2].wait_recv()
        out_ref[...] = jnp.maximum(best[0], result([1, 2, 3]))
        for c in back.values():
            c.wait_send()

    @pl.when(is_inner & jnp.logical_not(gives))
    def _():
        best_far[...] = jnp.full(best_far.shape, -1.0, jnp.float32)
        open_inner(False)
        for n in range(2):
            outer_arrived(n, False)
            lend[n].wait_recv()
            lend_on[n].start()
        cross_own.wait_recv()
        share_own[1].start()
        outer_arrived(2, False)
        settle([key_cross])
        key_share.start()
        cross_outer[0].wait_recv()
        share_outer[0].start()
        outer_arrived(3, False)
        outer_arrived(4, False)
        cross_outer[1].wait_recv()
        share_outer[1].start()
        load_rows.wait()
        settle([key_wide, key_pass, pass_own, wide] + pass_outer)
        columns(0, key_side, 2)
        columns(2, key_twin, 2)
        visit_half(near_tiles)
        settle(lend_on)
        share_own[0].start()
        cross_outer[2].wait_recv()
        share_outer[2].start()
        settle([key_share])
        columns(4, key_far, 4)
        visit_far(0, whole, near_tiles)
        settle(share_own)
        visit_far(2, whole, near_tiles)
        cross_outer[3].wait_recv()
        share_outer[3].start()
        settle(wide_outer + swing_up)
        visit_half(last_tile)
        visit_far(0, whole, last_tile)
        visit_far(2, whole, last_tile)
        cross_outer[4].wait_recv()
        share_outer[4].start()
        visit_far(1, whole, all_tiles)
        settle(share_outer[:3])
        visit_far(3, (0, 6), all_tiles)
        for slot in range(3):
            send_home(slot)
        settle(share_outer[3:])
        visit_far(3, (6, 2), all_tiles)
        send_back()
        send_home(3)
        for c in inner_sent + lend_on + share_own + share_outer + [key_share]:
            c.wait_send()
        back["inner"].wait_recv()
        out_ref[...] = jnp.maximum(best[0], result([1]))
        for c in home + list(back.values()):
            c.wait_send()


COPIES = 64


def kernel_body(embeddings, labels, member_rank):
    rows, width = embeddings.shape
    chunk = rows // PIECES
    dma = pltpu.SemaphoreType.DMA
    kept = embeddings.dtype
    out = pl.pallas_call(
        dedup_kernel,
        out_shape=pltpu.VMEM((1, rows), jnp.float32),
        in_specs=[pl.BlockSpec(memory_space=pl.ANY)] * 3,
        out_specs=pl.BlockSpec(memory_space=pltpu.VMEM),
        scratch_shapes=[
            pltpu.VMEM((4, rows, width), kept),
            pltpu.VMEM((2, rows, width), kept),
            pltpu.VMEM((4, rows, width), kept),
            pltpu.VMEM((rows // 2, width), kept),
            pltpu.VMEM((4, 2, 1, rows), jnp.int32),
            pltpu.VMEM((2, 2, 1, rows), jnp.int32),
            pltpu.VMEM((4, 2, 1, rows), jnp.int32),
            pltpu.VMEM((4, 1, rows), jnp.float32),
            pltpu.VMEM((4, rows, rows), jnp.float32),
            pltpu.VMEM((8, 1, rows), jnp.float32),
            pltpu.VMEM((4, 1, rows), jnp.float32),
            pltpu.VMEM((8, rows, rows), jnp.float32),
            pltpu.SemaphoreType.REGULAR((2,)),
            dma((3,)),
            dma((COPIES,)),
            dma((COPIES,)),
        ],
        compiler_params=pltpu.CompilerParams(collective_id=0, has_side_effects=True),
    )(embeddings, labels.reshape(1, rows), member_rank.reshape(1, rows))
    return out.reshape(rows)


def fits_kernel(rows):
    parts, clus, mem, sub = (lax.axis_size(a) for a in ("parts", "clus", "mem", "sub"))
    members = rows * clus * mem * sub
    clusters = CLUS_GROUP * clus * mem
    return (
        parts == mem == sub == PAIR
        and clus == 2 * PAIR
        and rows == LANES
        and members <= CLASS_STEP
        and clusters * CLASS_STEP <= EXACT
    )


def swapped(value, axis, stride):
    mask = 2**stride
    pairs = [(source, source ^ mask) for source in range(lax.axis_size(axis))]
    return lax.ppermute(value, axis, pairs)


def masked_best(row_emb, row_label, row_rank, col_emb, col_label, col_rank, want_columns):
    col_count = col_emb.shape[0]
    block_size = math.gcd(512, col_count)
    block_count = col_count // block_size
    emb_blocks = col_emb.reshape(block_count, block_size, col_emb.shape[1])
    label_blocks = col_label.reshape(block_count, block_size)
    rank_blocks = col_rank.reshape(block_count, block_size)

    def visit_block(running, column_piece):
        piece_emb, piece_label, piece_rank = column_piece
        scores = lax.dot_general(
            row_emb, piece_emb, (((1,), (1,)), ((), ())), preferred_element_type=jnp.float32
        )
        same_cluster = (row_label[:, None] == piece_label[None, :]) & (row_label[:, None] >= 0)
        earlier = piece_rank[None, :] < row_rank[:, None]
        row_best = jnp.max(jnp.where(same_cluster & earlier, scores, jnp.float32(-1.0)), axis=1)
        if want_columns:
            later = same_cluster & jnp.logical_not(earlier)
            col_best = jnp.max(jnp.where(later, scores, jnp.float32(-1.0)), axis=0)
        else:
            col_best = jnp.zeros((0,), jnp.float32)
        return (jnp.maximum(running, row_best), col_best)

    initial = jnp.full((row_emb.shape[0],), -1.0, jnp.float32)
    row_best, col_blocks = lax.scan(visit_block, initial, (emb_blocks, label_blocks, rank_blocks))
    return (row_best, col_blocks.reshape(-1))


def body(embeddings, labels, member_rank):
    row_count = embeddings.shape[0]
    feature_count = embeddings.shape[1]
    clus_count = lax.axis_size("clus")
    mem_count = lax.axis_size("mem")
    group_count = clus_count * mem_count
    capacity = 2 * row_count // group_count
    slot_count = group_count * capacity
    group_of = labels // CLUS_GROUP
    one_hot = (group_of[:, None] == jnp.arange(group_count, dtype=jnp.int32)[None, :]).astype(
        jnp.int32
    )
    running_count = jnp.cumsum(one_hot, axis=0) - 1
    within_group = jnp.sum(one_hot * running_count, axis=1)
    slot_of = group_of * capacity + within_group
    send_emb = jnp.zeros((slot_count, feature_count), jnp.bfloat16).at[slot_of].set(embeddings)
    send_label = jnp.full((slot_count,), -1, jnp.int32).at[slot_of].set(labels)
    send_rank = jnp.zeros((slot_count,), jnp.int32).at[slot_of].set(member_rank)
    received = (
        lax.all_to_all(
            send_emb.reshape(group_count, capacity, feature_count),
            ("clus", "mem"),
            split_axis=0,
            concat_axis=0,
            tiled=True,
        ),
        lax.all_to_all(
            send_label.reshape(group_count, capacity),
            ("clus", "mem"),
            split_axis=0,
            concat_axis=0,
            tiled=True,
        ),
        lax.all_to_all(
            send_rank.reshape(group_count, capacity),
            ("clus", "mem"),
            split_axis=0,
            concat_axis=0,
            tiled=True,
        ),
    )
    own_emb = received[0].reshape(slot_count, feature_count)
    own_label = received[1].reshape(slot_count)
    own_rank = received[2].reshape(slot_count)
    other_emb, other_label, other_rank = swapped((own_emb, own_label, own_rank), "sub", 0)
    diag_best, ignored = masked_best(
        own_emb, own_label, own_rank, own_emb, own_label, own_rank, False
    )
    core_side = lax.axis_index("sub")
    is_zero = core_side == 0
    zero_emb = jnp.where(is_zero, own_emb, other_emb)
    zero_label = jnp.where(is_zero, own_label, other_label)
    zero_rank = jnp.where(is_zero, own_rank, other_rank)
    one_emb = jnp.where(is_zero, other_emb, own_emb)
    one_label = jnp.where(is_zero, other_label, own_label)
    one_rank = jnp.where(is_zero, other_rank, own_rank)
    half_count = slot_count // 2
    offset = core_side * half_count
    part_emb = lax.dynamic_slice_in_dim(zero_emb, offset, half_count, 0)
    part_label = lax.dynamic_slice_in_dim(zero_label, offset, half_count, 0)
    part_rank = lax.dynamic_slice_in_dim(zero_rank, offset, half_count, 0)
    half_best, col_part = masked_best(
        part_emb, part_label, part_rank, one_emb, one_label, one_rank, True
    )
    got_half, got_cols = swapped((half_best, col_part), "sub", 0)
    row_side = jnp.concatenate([half_best, got_half])
    cross_best = jnp.where(is_zero, row_side, jnp.maximum(col_part, got_cols))
    nearest = jnp.maximum(diag_best, cross_best)
    returned = lax.all_to_all(
        nearest.reshape(group_count, capacity),
        ("clus", "mem"),
        split_axis=0,
        concat_axis=0,
        tiled=True,
    )
    return returned.reshape(-1)[slot_of]


def local(embeddings, labels, member_rank):
    if fits_kernel(embeddings.shape[0]):
        return kernel_body(embeddings, labels, member_rank)
    return body(embeddings, labels, member_rank)


def solution(mesh):
    placed = (
        P(("parts", "clus", "mem", "sub"), None),
        P(("parts", "clus", "mem", "sub")),
        P(("parts", "clus", "mem", "sub")),
    )
    return jax.shard_map(
        local,
        mesh=mesh,
        in_specs=placed,
        out_specs=P(("parts", "clus", "mem", "sub")),
        check_vma=False,
    )
```

```python
import functools
import math

import jax
import jax.numpy as jnp
from jax import lax
from jax.experimental import pallas as pl
from jax.experimental.pallas import tpu as pltpu
from jax.sharding import PartitionSpec as P

CLUS_GROUP = 2
MESH = pl.DeviceIdType.MESH
LANES = 128
PAIR = 2
PIECES = 8
CLASS_STEP = 65536
EXACT = 2**24


def nt_dot(lhs, rhs):
    return lax.dot_general(lhs, rhs, (((1,), (1,)), ((), ())), preferred_element_type=jnp.float32)


def dedup_kernel(
    emb_hbm,
    label_hbm,
    rank_hbm,
    out_ref,
    side,
    twin,
    far_rows,
    relay,
    key_side,
    key_twin,
    key_far,
    best,
    best_far,
    ret_out,
    ret_in,
    key_column,
    entered,
    load_sem,
    send_sem,
    recv_sem,
):
    rows, _ = emb_hbm.shape
    chunk = rows // PIECES
    part = lax.axis_index("parts")
    clus = lax.axis_index("clus")
    mem = lax.axis_index("mem")
    sub = lax.axis_index("sub")
    clus_count = lax.axis_size("clus")
    parity = lax.rem(clus, 2)
    along = clus + 1 - 2 * parity
    across = clus_count - 1 - clus
    beyond = clus_count - 1 - along
    is_inner = (clus >= 1) & (clus < clus_count - 1)
    gives = lax.div(clus, 2) != part
    to_along = {"clus": along}
    to_across = {"clus": across}
    to_column = {"mem": 1 - mem}
    to_twin = {"sub": 1 - sub}
    to_part = {"parts": 1 - part}

    used = {}

    def copy(name, src, dst, device):
        slot = used.setdefault(name, len(used))
        return pltpu.make_async_remote_copy(
            src_ref=src,
            dst_ref=dst,
            send_sem=send_sem.at[slot],
            recv_sem=recv_sem.at[slot],
            device_id=device,
            device_id_type=MESH,
        )

    def span(k, count=1):
        return pl.ds(k * chunk, count * chunk)

    def piece(ref, slot, k, count=1):
        return ref.at[slot, span(k, count), :]

    load_label = pltpu.make_async_copy(label_hbm, key_side.at[0, 0], load_sem.at[0])
    load_rank = pltpu.make_async_copy(rank_hbm, key_side.at[0, 1], load_sem.at[1])
    load_rows = pltpu.make_async_copy(emb_hbm, side.at[0], load_sem.at[2])

    half = PIECES // 2
    steps = [(0, 2), (2, 2), (4, 2), (6, 1), (7, 1)]
    low_steps = steps[:2]
    high_steps = [(4, 2), (6, 2)]

    def rows_of(step):
        return emb_hbm.at[span(*step), :]

    key_up = [
        copy("label_up", label_hbm, key_side.at[1, 0], to_along),
        copy("rank_up", rank_hbm, key_side.at[1, 1], to_along),
    ]
    up = [copy(("up", t), rows_of(t), piece(side, 1, *t), to_along) for t in steps]
    swing = [copy(("swing", t), rows_of(t), piece(side, 3, *t), to_column) for t in high_steps]
    swing_up = [
        copy(("swing_up", t), piece(side, 3, *t), piece(side, 3, *t), to_along) for t in high_steps
    ]
    wide = copy("wide", emb_hbm, side.at[2], to_column)
    wide_outer = [
        copy(("wide_outer", t), piece(side, 1, *t), piece(side, 3, *t), to_column)
        for t in low_steps
    ]
    key_wide = copy("key_wide", key_side.at[pl.ds(0, 2)], key_side.at[pl.ds(2, 2)], to_column)
    pass_own = copy("pass_own", emb_hbm, twin.at[0], to_twin)
    pass_outer = [
        copy(("pass_outer", t), piece(side, 1, *t), piece(twin, 1, *t), to_twin) for t in steps
    ]
    key_pass = copy("key_pass", key_side.at[pl.ds(0, 2)], key_twin, to_twin)
    upper = (half, half)
    lower = (0, half)
    cross_own = copy("cross_own", rows_of(upper), piece(far_rows, 0, *upper), to_across)
    cross_outer = [
        copy(("cross_outer", t), piece(side, 1, *t), piece(far_rows, 1, *t), to_across)
        for t in steps
    ]
    key_cross = copy("key_cross", key_side.at[pl.ds(0, 2)], key_far.at[pl.ds(0, 2)], to_across)
    lend = [copy(("lend", t), rows_of(t), relay.at[span(*t), :], to_part) for t in low_steps]
    lend_on = [
        copy(
            ("lend_on", t),
            relay.at[span(*t), :],
            piece(far_rows, 0, *t),
            {"parts": 1 - part, "clus": across},
        )
        for t in low_steps
    ]
    share_own = [
        copy(("share_own", t), piece(far_rows, 0, *t), piece(far_rows, 2, *t), to_twin)
        for t in (lower, upper)
    ]
    share_outer = [
        copy(("share_outer", t), piece(far_rows, 1, *t), piece(far_rows, 3, *t), to_twin)
        for t in steps
    ]
    key_share = copy("key_share", key_far.at[pl.ds(0, 2)], key_far.at[pl.ds(2, 2)], to_twin)
    back = {
        "outer": copy("back_outer", ret_out.at[1], ret_in.at[0], to_along),
        "inner": copy("back_inner", ret_out.at[2], ret_in.at[1], to_column),
        "outer_wide": copy(
            "back_outer_wide", ret_out.at[3], ret_in.at[1], {"clus": along, "mem": 1 - mem}
        ),
    }
    home = [
        copy("home_0", ret_out.at[4], ret_in.at[2], to_across),
        copy("home_1", ret_out.at[5], ret_in.at[2], {"clus": beyond}),
        copy("home_2", ret_out.at[6], ret_in.at[3], {"clus": across, "sub": 1 - sub}),
        copy("home_3", ret_out.at[7], ret_in.at[3], {"clus": beyond, "sub": 1 - sub}),
    ]

    barrier = pltpu.get_barrier_semaphore()

    def greet(devices):
        for device in devices:
            pl.semaphore_signal(barrier, inc=1, device_id=device, device_id_type=MESH)
        return len(devices)

    def key_of(ref, slot):
        return (ref[slot, 0] * CLASS_STEP + ref[slot, 1]).astype(jnp.float32)

    def cluster(key):
        return jnp.floor(key * (1.0 / CLASS_STEP))

    def columns(first, ref, slots):
        for n in range(slots):
            key = jnp.broadcast_to(key_of(ref, n), (LANES, rows))
            key_column[first + n] = jnp.transpose(key)

    def visit(source, slot, first_key, step, tiles, reversed_too=False):
        place = span(*step)
        cand_key = key_column[first_key + slot, place, :]
        cand_cluster = cluster(cand_key)
        members = side[tiles[0] : tiles[-1] + 1].reshape(len(tiles) * rows, side.shape[2])
        scores = nt_dot(source[slot, place, :], members)
        reverse = None
        for n, tile in enumerate(tiles):
            score = scores[:, n * rows : (n + 1) * rows]
            member_key = key_of(key_side, tile)
            same = cand_cluster == cluster(member_key)
            earlier = same & (cand_key < member_key)
            top = jnp.max(jnp.where(earlier, score, -1.0), axis=0, keepdims=True)
            best[tile] = jnp.maximum(best[tile], top)
            if reversed_too:
                later = jnp.where(same & (cand_key > member_key), score, -1.0)
                reverse = later if reverse is None else jnp.maximum(reverse, later)
        if reversed_too:
            best_far[slot, place, :] = jnp.maximum(best_far[slot, place, :], reverse)

    def visit_far(slot, step, tiles):
        visit(far_rows, slot, 4, step, tiles, True)

    def visit_one(source, first_key, tiles):
        width = side.shape[2]
        cand_key = key_column[first_key : first_key + 2].reshape(2 * rows, rows)
        cand_cluster = cluster(cand_key)
        members = side[tiles[0] : tiles[-1] + 1].reshape(len(tiles) * rows, width)
        scores = nt_dot(source[0:2].reshape(2 * rows, width), members)
        for n, tile in enumerate(tiles):
            member_key = key_of(key_side, tile)
            earlier = (cand_cluster == cluster(member_key)) & (cand_key < member_key)
            score = jnp.where(earlier, scores[:, n * rows : (n + 1) * rows], -1.0)
            best[tile] = jnp.maximum(best[tile], jnp.max(score, axis=0, keepdims=True))

    def visit_half(tiles):
        visit_one(side, 0, tiles)
        visit_one(twin, 2, tiles)

    def open_inner(gives_here):
        load_label.start()
        load_rank.start()
        load_rows.start()
        met = greet([to_along, to_across, to_column, to_twin, to_part])
        best[...] = jnp.full(best.shape, -1.0, jnp.float32)
        pl.semaphore_wait(barrier, met)
        pl.semaphore_signal(entered.at[0], inc=1, device_id=to_column, device_id_type=MESH)
        if gives_here:
            cross_own.start()
            for c in lend:
                c.start()
        wide.start()
        pass_own.start()
        pl.semaphore_wait(entered.at[0], 1)
        pl.semaphore_signal(entered.at[1], inc=1, device_id=to_along, device_id_type=MESH)
        load_label.wait()
        load_rank.wait()
        settle(key_up)
        if gives_here:
            key_cross.start()
        key_pass.start()
        key_wide.start()

    def outer_arrived(n, gives_here):
        up[n].wait_recv()
        if gives_here:
            cross_outer[n].start()
        if n < len(low_steps):
            wide_outer[n].start()
        pass_outer[n].start()

    def settle(copies):
        for c in copies:
            c.wait_recv()

    inner_sent = wide_outer + pass_outer + [wide, pass_own, key_wide, key_pass]
    whole = (0, PIECES)

    def result(slots):
        value = ret_in[slots[0]]
        for slot in slots[1:]:
            value = jnp.maximum(value, ret_in[slot])
        return value

    def send_home(slot):
        ret_out[4 + slot] = jnp.max(jnp.transpose(best_far[slot]), axis=0, keepdims=True)
        home[slot].start()

    near_tiles = [0, 1, 2]
    last_tile = [3]
    all_tiles = near_tiles + last_tile

    def send_back():
        for tile, name in ((3, "outer_wide"), (1, "outer"), (2, "inner")):
            ret_out[tile] = best[tile]
            back[name].start()

    @pl.when(jnp.logical_not(is_inner))
    def _():
        met = greet([to_along])
        pl.semaphore_wait(barrier, met)
        for c in key_up + up:
            c.start()
        pl.semaphore_wait(entered.at[1], 1)
        for c in swing:
            c.start()
        for c, onward in zip(swing, swing_up, strict=True):
            c.wait_recv()
            onward.start()
        for c in key_up + up + swing + swing_up:
            c.wait_send()
        back["outer"].wait_recv()
        back["outer_wide"].wait_recv()

        @pl.when(gives)
        def _():
            home[1].wait_recv()
            home[3].wait_recv()
            out_ref[...] = result([0, 1, 2, 3])

        @pl.when(jnp.logical_not(gives))
        def _():
            out_ref[...] = result([0, 1])

    @pl.when(is_inner & gives)
    def _():
        open_inner(True)
        for n in range(len(steps)):
            outer_arrived(n, True)
        load_rows.wait()
        settle([key_wide, key_pass, pass_own, wide] + pass_outer)
        columns(0, key_side, 2)
        columns(2, key_twin, 2)
        settle(wide_outer + swing_up)
        visit_half(all_tiles)
        send_back()
        for c in inner_sent + lend + cross_outer + [cross_own, key_cross]:
            c.wait_send()
        back["inner"].wait_recv()
        home[0].wait_recv()
        home[2].wait_recv()
        out_ref[...] = jnp.maximum(best[0], result([1, 2, 3]))
        for c in back.values():
            c.wait_send()

    @pl.when(is_inner & jnp.logical_not(gives))
    def _():
        best_far[...] = jnp.full(best_far.shape, -1.0, jnp.float32)
        open_inner(False)
        columns(0, key_side, 2)
        load_rows.wait()
        for n in range(2):
            outer_arrived(n, False)
            lend[n].wait_recv()
            lend_on[n].start()
        cross_own.wait_recv()
        share_own[1].start()
        settle([key_cross])
        key_share.start()
        outer_arrived(2, False)
        cross_outer[0].wait_recv()
        share_outer[0].start()
        outer_arrived(3, False)
        outer_arrived(4, False)
        visit_one(side, 0, [0, 1])
        cross_outer[1].wait_recv()
        share_outer[1].start()
        settle([key_pass, pass_own] + pass_outer)
        columns(2, key_twin, 2)
        visit_one(twin, 2, [0, 1])
        settle(lend_on)
        share_own[0].start()
        settle([key_wide, wide])
        visit_half([2])
        cross_outer[2].wait_recv()
        share_outer[2].start()
        settle([key_share])
        columns(4, key_far, 4)
        visit_far(0, whole, near_tiles)
        cross_outer[3].wait_recv()
        share_outer[3].start()
        settle(share_own)
        visit_far(2, whole, near_tiles)
        cross_outer[4].wait_recv()
        share_outer[4].start()
        settle(wide_outer + swing_up)
        visit_half(last_tile)
        visit_far(0, whole, last_tile)
        visit_far(2, whole, last_tile)
        visit_far(1, whole, all_tiles)
        settle(share_outer[:3])
        visit_far(3, (0, 6), all_tiles)
        settle(share_outer[3:])
        visit_far(3, (6, 2), all_tiles)
        send_back()
        for slot in (1, 3, 0, 2):
            send_home(slot)
        for c in inner_sent + lend_on + share_own + share_outer + [key_share]:
            c.wait_send()
        back["inner"].wait_recv()
        out_ref[...] = jnp.maximum(best[0], result([1]))
        for c in home + list(back.values()):
            c.wait_send()


COPIES = 64


def kernel_body(embeddings, labels, member_rank):
    rows, width = embeddings.shape
    chunk = rows // PIECES
    dma = pltpu.SemaphoreType.DMA
    kept = embeddings.dtype
    out = pl.pallas_call(
        dedup_kernel,
        out_shape=pltpu.VMEM((1, rows), jnp.float32),
        in_specs=[pl.BlockSpec(memory_space=pl.ANY)] * 3,
        out_specs=pl.BlockSpec(memory_space=pltpu.VMEM),
        scratch_shapes=[
            pltpu.VMEM((4, rows, width), kept),
            pltpu.VMEM((2, rows, width), kept),
            pltpu.VMEM((4, rows, width), kept),
            pltpu.VMEM((rows // 2, width), kept),
            pltpu.VMEM((4, 2, 1, rows), jnp.int32),
            pltpu.VMEM((2, 2, 1, rows), jnp.int32),
            pltpu.VMEM((4, 2, 1, rows), jnp.int32),
            pltpu.VMEM((4, 1, rows), jnp.float32),
            pltpu.VMEM((4, rows, rows), jnp.float32),
            pltpu.VMEM((8, 1, rows), jnp.float32),
            pltpu.VMEM((4, 1, rows), jnp.float32),
            pltpu.VMEM((8, rows, rows), jnp.float32),
            pltpu.SemaphoreType.REGULAR((2,)),
            dma((3,)),
            dma((COPIES,)),
            dma((COPIES,)),
        ],
        compiler_params=pltpu.CompilerParams(collective_id=0, has_side_effects=True),
    )(embeddings, labels.reshape(1, rows), member_rank.reshape(1, rows))
    return out.reshape(rows)


def fits_kernel(rows):
    parts, clus, mem, sub = (lax.axis_size(a) for a in ("parts", "clus", "mem", "sub"))
    members = rows * clus * mem * sub
    clusters = CLUS_GROUP * clus * mem
    return (
        parts == mem == sub == PAIR
        and clus == 2 * PAIR
        and rows == LANES
        and members <= CLASS_STEP
        and clusters * CLASS_STEP <= EXACT
    )


def swapped(value, axis, stride):
    mask = 2**stride
    pairs = [(source, source ^ mask) for source in range(lax.axis_size(axis))]
    return lax.ppermute(value, axis, pairs)


def masked_best(row_emb, row_label, row_rank, col_emb, col_label, col_rank, want_columns):
    col_count = col_emb.shape[0]
    block_size = math.gcd(512, col_count)
    block_count = col_count // block_size
    emb_blocks = col_emb.reshape(block_count, block_size, col_emb.shape[1])
    label_blocks = col_label.reshape(block_count, block_size)
    rank_blocks = col_rank.reshape(block_count, block_size)

    def visit_block(running, column_piece):
        piece_emb, piece_label, piece_rank = column_piece
        scores = lax.dot_general(
            row_emb, piece_emb, (((1,), (1,)), ((), ())), preferred_element_type=jnp.float32
        )
        same_cluster = (row_label[:, None] == piece_label[None, :]) & (row_label[:, None] >= 0)
        earlier = piece_rank[None, :] < row_rank[:, None]
        row_best = jnp.max(jnp.where(same_cluster & earlier, scores, jnp.float32(-1.0)), axis=1)
        if want_columns:
            later = same_cluster & jnp.logical_not(earlier)
            col_best = jnp.max(jnp.where(later, scores, jnp.float32(-1.0)), axis=0)
        else:
            col_best = jnp.zeros((0,), jnp.float32)
        return (jnp.maximum(running, row_best), col_best)

    initial = jnp.full((row_emb.shape[0],), -1.0, jnp.float32)
    row_best, col_blocks = lax.scan(visit_block, initial, (emb_blocks, label_blocks, rank_blocks))
    return (row_best, col_blocks.reshape(-1))


def body(embeddings, labels, member_rank):
    row_count = embeddings.shape[0]
    feature_count = embeddings.shape[1]
    clus_count = lax.axis_size("clus")
    mem_count = lax.axis_size("mem")
    group_count = clus_count * mem_count
    capacity = 2 * row_count // group_count
    slot_count = group_count * capacity
    group_of = labels // CLUS_GROUP
    one_hot = (group_of[:, None] == jnp.arange(group_count, dtype=jnp.int32)[None, :]).astype(
        jnp.int32
    )
    running_count = jnp.cumsum(one_hot, axis=0) - 1
    within_group = jnp.sum(one_hot * running_count, axis=1)
    slot_of = group_of * capacity + within_group
    send_emb = jnp.zeros((slot_count, feature_count), jnp.bfloat16).at[slot_of].set(embeddings)
    send_label = jnp.full((slot_count,), -1, jnp.int32).at[slot_of].set(labels)
    send_rank = jnp.zeros((slot_count,), jnp.int32).at[slot_of].set(member_rank)
    received = (
        lax.all_to_all(
            send_emb.reshape(group_count, capacity, feature_count),
            ("clus", "mem"),
            split_axis=0,
            concat_axis=0,
            tiled=True,
        ),
        lax.all_to_all(
            send_label.reshape(group_count, capacity),
            ("clus", "mem"),
            split_axis=0,
            concat_axis=0,
            tiled=True,
        ),
        lax.all_to_all(
            send_rank.reshape(group_count, capacity),
            ("clus", "mem"),
            split_axis=0,
            concat_axis=0,
            tiled=True,
        ),
    )
    own_emb = received[0].reshape(slot_count, feature_count)
    own_label = received[1].reshape(slot_count)
    own_rank = received[2].reshape(slot_count)
    other_emb, other_label, other_rank = swapped((own_emb, own_label, own_rank), "sub", 0)
    diag_best, ignored = masked_best(
        own_emb, own_label, own_rank, own_emb, own_label, own_rank, False
    )
    core_side = lax.axis_index("sub")
    is_zero = core_side == 0
    zero_emb = jnp.where(is_zero, own_emb, other_emb)
    zero_label = jnp.where(is_zero, own_label, other_label)
    zero_rank = jnp.where(is_zero, own_rank, other_rank)
    one_emb = jnp.where(is_zero, other_emb, own_emb)
    one_label = jnp.where(is_zero, other_label, own_label)
    one_rank = jnp.where(is_zero, other_rank, own_rank)
    half_count = slot_count // 2
    offset = core_side * half_count
    part_emb = lax.dynamic_slice_in_dim(zero_emb, offset, half_count, 0)
    part_label = lax.dynamic_slice_in_dim(zero_label, offset, half_count, 0)
    part_rank = lax.dynamic_slice_in_dim(zero_rank, offset, half_count, 0)
    half_best, col_part = masked_best(
        part_emb, part_label, part_rank, one_emb, one_label, one_rank, True
    )
    got_half, got_cols = swapped((half_best, col_part), "sub", 0)
    row_side = jnp.concatenate([half_best, got_half])
    cross_best = jnp.where(is_zero, row_side, jnp.maximum(col_part, got_cols))
    nearest = jnp.maximum(diag_best, cross_best)
    returned = lax.all_to_all(
        nearest.reshape(group_count, capacity),
        ("clus", "mem"),
        split_axis=0,
        concat_axis=0,
        tiled=True,
    )
    return returned.reshape(-1)[slot_of]


def local(embeddings, labels, member_rank):
    if fits_kernel(embeddings.shape[0]):
        return kernel_body(embeddings, labels, member_rank)
    return body(embeddings, labels, member_rank)


def solution(mesh):
    placed = (
        P(("parts", "clus", "mem", "sub"), None),
        P(("parts", "clus", "mem", "sub")),
        P(("parts", "clus", "mem", "sub")),
    )
    return jax.shard_map(
        local,
        mesh=mesh,
        in_specs=placed,
        out_specs=P(("parts", "clus", "mem", "sub")),
        check_vma=False,
    )
```
